256 devices in a mesh: row: 16 (over z, y_lo), col: 16 (over x, y_hi, core).
Axes of the slice: x: 4, y: 4 (y_hi: 2, y_lo: 2; y = y_hi * 2 + y_lo), z: 8, core: 2. Of those that a mesh axis runs over, the one named last changes fastest.
Arguments:
- kernels: bfloat16 [7, 12288, 12288], P(None, 'row', 'col'), may hold values from -0.02734375 to 0.02734375
- prestress: float32 [4, 12288, 512], P(None, 'row'), may hold values from -6 to 6
- rates_hist: bfloat16 [4, 12288, 512], P(None, 'col'), may hold values from -1 to 1
- gain: float32 [12288], P('row'), may hold values from 0.3 to 3
Outputs:
- rates: bfloat16 [4, 12288, 512], P(None, 'col', 'row')
- tractions: float32 [4, 12288, 512], P(None, 'row', 'col')
The draws below stay inside these ranges and needn't reach their ends.
All inputs are finite; a program needn't handle non-finite values.
Results may differ from the reference program's by a relative error of at most 0.0018.
Values may be sent and summed in bfloat16 or wider, within the bound.
No kernel may reach another device: no remote copies, remote signals or barrier semaphores. Data moves between devices by JAX's collectives and lax.ppermute only.
A program may use at most 128 MiB of HBM per device.

```python
import math
import jax
import jax.numpy as jnp

N = 12288
S = 512
STEPS = 4
HIST = 4
DEL = 7


def levels(stream_key, extent, pieces, smallest, high):
    def one(dim, parts):
        steps = jax.random.uniform(jax.random.fold_in(jax.random.fold_in(stream_key, 6), dim), (parts,), jnp.float32, smallest / len(pieces), high / len(pieces))
        return jnp.repeat(jnp.exp(steps), extent[dim] // parts).reshape((-1,) + (1,) * (len(extent) - dim - 1))

    level = one(*pieces[0])
    for cut in pieces[1:]:
        level = level * one(*cut)
    return level


def gaussian(own_key, shape, scale, bound, pieces=(), held_as=jnp.bfloat16):
    values = jax.random.normal(own_key, shape, jnp.float32) * scale
    if len(pieces) > 0:
        values = levels(own_key, shape, pieces, -0.22, 0.18) * values
    return jnp.clip(values, min=-bound, max=bound).astype(held_as)


def setup_inputs(seed: int = 0) -> dict:
    arg_keys = jax.random.split(jax.random.key(seed), 5)
    kernels = gaussian(arg_keys[0], (DEL, N, N), (4 * N) ** -0.5, 0.02734375, ((1, 16), (2, 16)))
    prestress = gaussian(arg_keys[1], (STEPS, N, S), 1.0, 6.0, ((1, 16),), jnp.float32)
    rates_hist = jnp.clip(jax.random.uniform(arg_keys[2], (HIST, N, S), jnp.float32, -1.0, 1.0) * levels(arg_keys[2], (HIST, N, S), ((1, 16),), -0.4, 0.0), -1.0, 1.0).astype(jnp.bfloat16)
    gain = jnp.clip(jnp.exp(math.log(3.0) - 2.3025851 * jax.random.uniform(arg_keys[3], (N,), jnp.float32) ** levels(arg_keys[3], (N,), ((0, 16),), -0.2, 0.2)), 0.3, 3.0)
    return {"kernels": kernels, "prestress": prestress, "rates_hist": rates_hist, "gain": gain}


def reference(kernels, prestress, rates_hist, gain):
    stored = [rates_hist[position] for position in range(HIST)]
    rate_list = []
    traction_list = []
    for moment in range(1, STEPS + 1):
        traction = prestress[moment - 1]
        for offset in range(1, moment + HIST):
            traction = traction + jnp.dot(kernels[offset - 1], stored[HIST - 1 + moment - offset], preferred_element_type=jnp.float32)
        slip_rate = jnp.tanh(gain[:, None] * traction).astype(jnp.bfloat16)
        stored.append(slip_rate)
        rate_list.append(slip_rate)
        traction_list.append(traction)
    return jnp.stack(rate_list), jnp.stack(traction_list)
```

```python
import jax
import jax.numpy as jnp
from jax import lax
from jax.sharding import Mesh
from jax.sharding import PartitionSpec as P

AXES = ("z", "yl", "x", "yh", "k")
SIZES = (8, 2, 4, 2, 2)
ROW = ("z", "yl")
CHIP = ("x", "yh")
COL = ("x", "yh", "k")


def pairs_of(move):
    def number(place):
        total = 0
        for size, at in zip(SIZES, place):
            total = total * size + at
        return total

    found = []
    for z in range(8):
        for yl in range(2):
            for u in range(8):
                for k in range(2):
                    to_z, to_yl, to_u, to_k = move(z, yl, u, k)
                    source = (z, yl, u // 2, u % 2, k)
                    target = (to_z, to_yl, to_u // 2, to_u % 2, to_k)
                    found.append((number(source), number(target)))
    return found


def moved(array, move):
    return lax.ppermute(array, AXES, pairs_of(move))


def other_core(array):
    return moved(array, lambda z, yl, u, k: (z, yl, u, 1 - k))


def by_scenario(rates, kernel):
    return lax.dot_general(
        rates, kernel, (((1,), (1,)), ((), ())), preferred_element_type=jnp.float32
    )


def per_device(kernels, prestress, rates_hist, gain):
    moments, rows, scen = prestress.shape
    history = rates_hist.shape[0]
    share = scen // 16
    core = lax.axis_index("k")
    my_col = lax.axis_index(COL)

    load = lax.dynamic_slice_in_dim(prestress, my_col * share, share, 2)
    load = jnp.swapaxes(load, 1, 2)

    def two_tiles(kernel):
        theirs = other_core(kernel)
        first = jnp.where(core == 0, kernel, theirs)
        second = jnp.where(core == 0, theirs, kernel)
        return first, second

    def known(moment):
        total = 0.0
        for offset in range(moment, moment + history):
            total = total + lax.dot_general(
                rates_hist[history - 1 + moment - offset],
                kernels[offset - 1],
                (((0,), (1,)), ((), ())),
                preferred_element_type=jnp.float32,
            )
        total = total.reshape(8, 2, share, rows)
        mine = lax.dynamic_index_in_dim(total, core, 1, keepdims=False)
        theirs = lax.dynamic_index_in_dim(total, 1 - core, 1, keepdims=False)
        return mine + other_core(theirs)

    tiles = [two_tiles(kernels[position]) for position in range(moments - 1)]
    known_parts = [known(moment) for moment in range(1, moments + 1)]
    gathered = []
    traction_list = []
    crossed_list = []
    last_rates = None
    for moment in range(1, moments + 1):
        partial_value = known_parts[moment - 1]
        for back in range(1, moment):
            first, second = tiles[back - 1]
            one, two = gathered[moment - back - 1]
            extra = by_scenario(one, first) + by_scenario(two, second)
            partial_value = partial_value + extra.reshape(partial_value.shape)
        arrived = lax.all_to_all(partial_value, CHIP, 0, 0, tiled=True)
        traction = arrived.sum(axis=0) + load[moment - 1]
        traction_list.append(traction)
        rate = jnp.tanh(gain[None, :] * traction).astype(jnp.bfloat16)
        if moment < moments:
            crossed = moved(rate, lambda z, yl, u, k: (u, yl, z, k))
            crossed_list.append(crossed)
            copies = jnp.broadcast_to(crossed, (16, *crossed.shape))
            joined = lax.all_to_all(copies, ROW, 0, 0, tiled=True)
            joined = joined.reshape(8, 2, share, rows)
            gathered.append(
                (joined[:, 0].reshape(8 * share, rows), joined[:, 1].reshape(8 * share, rows))
            )
        else:
            last_rates = moved(rate, lambda z, yl, u, k: (u, k, z, yl))
    early = moved(jnp.stack(crossed_list), lambda z, yl, u, k: (z, k, u, yl))
    rates = jnp.concatenate([early, last_rates[None]], axis=0)
    tractions = jnp.stack(traction_list)
    return jnp.swapaxes(rates, 1, 2), jnp.swapaxes(tractions, 1, 2)


def solution(mesh):
    finer = Mesh(mesh.devices.reshape(SIZES), AXES)
    return jax.shard_map(
        per_device,
        mesh=finer,
        in_specs=(P(None, ROW, COL), P(None, ROW, None), P(None, COL, None), P(ROW)),
        out_specs=(P(None, COL, ROW), P(None, ROW, COL)),
        check_vma=False,
    )
```

```python
import jax
import jax.numpy as jnp
from jax import lax
from jax.experimental import pallas as pl
from jax.experimental.pallas import tpu as pltpu
from jax.sharding import Mesh
from jax.sharding import PartitionSpec as P

AXES = ("z", "yl", "x", "yh", "k")
SIZES = (8, 2, 4, 2, 2)
ROW = ("z", "yl")
CHIP = ("x", "yh")
COL = ("x", "yh", "k")
PLACE = tuple((u + 4) % 8 for u in range(8))


def pairs_of(move):
    def number(place):
        total = 0
        for size, at in zip(SIZES, place):
            total = total * size + at
        return total

    found = []
    for z in range(8):
        for yl in range(2):
            for u in range(8):
                for k in range(2):
                    to_z, to_yl, to_u, to_k = move(z, yl, u, k)
                    source = (z, yl, u // 2, u % 2, k)
                    target = (to_z, to_yl, to_u // 2, to_u % 2, to_k)
                    found.append((number(source), number(target)))
    return found


def moved(array, move):
    return lax.ppermute(array, AXES, pairs_of(move))


def other_core(array):
    return moved(array, lambda z, yl, u, k: (z, yl, u, 1 - k))


def other_half(array):
    return moved(array, lambda z, yl, u, k: (z, 1 - yl, u, k))


def times(rates, kernel):
    return lax.dot_general(
        rates, kernel, (((1,), (1,)), ((), ())), preferred_element_type=jnp.float32
    )


def known_kernel(core_ref, kernel_ref, rates_ref, mine_ref, theirs_ref, total, turned):
    step = pl.program_id(0)
    product = jnp.dot(kernel_ref[0], rates_ref[0], preferred_element_type=jnp.float32)

    @pl.when(step == 0)
    def _():
        total[...] = product

    @pl.when(step > 0)
    def _():
        total[...] += product

    @pl.when(step == pl.num_programs(0) - 1)
    def _():
        turned[...] = total[...].T
        core = core_ref[0]
        share = mine_ref.shape[1]
        for u in range(mine_ref.shape[0]):
            start = pl.multiple_of((2 * u + core) * share, share)
            mine_ref[u] = turned[pl.ds(start, share), :]
            start = pl.multiple_of((2 * u + 1 - core) * share, share)
            theirs_ref[u] = turned[pl.ds(start, share), :]


def known(kernels, rates_hist, core, moment):
    history, rows, scen = rates_hist.shape
    share = scen // 16
    out = jax.ShapeDtypeStruct((8, share, rows), jnp.float32)
    return pl.pallas_call(
        known_kernel,
        grid_spec=pltpu.PrefetchScalarGridSpec(
            num_scalar_prefetch=1,
            grid=(history,),
            in_specs=[
                pl.BlockSpec((1, rows, rows), lambda q, c: (moment - 1 + q, 0, 0)),
                pl.BlockSpec((1, rows, scen), lambda q, c: (history - 1 - q, 0, 0)),
            ],
            out_specs=[
                pl.BlockSpec((8, share, rows), lambda q, c: (0, 0, 0)),
                pl.BlockSpec((8, share, rows), lambda q, c: (0, 0, 0)),
            ],
            scratch_shapes=[
                pltpu.VMEM((rows, scen), jnp.float32),
                pltpu.VMEM((scen, rows), jnp.float32),
            ],
        ),
        out_shape=[out, out],
        cost_estimate=pl.CostEstimate(
            flops=2 * history * rows * rows * scen,
            bytes_accessed=2 * history * rows * (rows + scen) + 4 * rows * scen,
            transcendentals=0,
        ),
        name="known",
    )(core.reshape(1).astype(jnp.int32), kernels, rates_hist)


def per_device(kernels, prestress, rates_hist, gain):
    moments, rows, scen = prestress.shape
    share = scen // 16
    half = share // 2
    core = lax.axis_index("k")
    yl = lax.axis_index("yl")
    chip = lax.axis_index(CHIP)
    plane = lax.axis_index("z")
    where = (core, yl, chip, plane)

    def after(value):
        return lax.optimization_barrier((where, value))

    def load_at(place, moment):
        core, _, chip, _ = place
        start = (2 * chip + core) * share
        load = lax.dynamic_slice(prestress, (moment - 1, 0, start), (1, rows, share))
        return load[0].T

    def halves(array, axis, yl):
        keep = lax.dynamic_slice_in_dim(array, yl * half, half, axis)
        send = lax.dynamic_slice_in_dim(array, (1 - yl) * half, half, axis)
        return keep, send

    def in_order(keep, got, flag):
        return jnp.concatenate([jnp.where(flag, got, keep), jnp.where(flag, keep, got)], axis=-2)

    def known_halves(place, moment):
        core, yl, chip, _ = place
        mine, theirs = known(kernels, rates_hist, core, moment)
        mine_only = (jnp.arange(8) == chip).astype(jnp.float32)[:, None, None]
        base = mine + other_core(theirs) + mine_only * load_at(place, moment)
        return lax.optimization_barrier(halves(base, 1, yl))

    def tiles_first(joined, same):
        one, two = joined[..., :rows], joined[..., rows:]
        one, two = jnp.where(same, one, two), jnp.where(same, two, one)
        return one.reshape(8 * half, rows), two.reshape(8 * half, rows)

    def summed(partial_value):
        return lax.all_to_all(partial_value, CHIP, 0, 0, tiled=True).sum(axis=0)

    def spread(piece):
        return moved(piece, lambda z, yl, u, k: (PLACE[u], yl, z, k))

    def joined_from(crossed):
        copies = jnp.broadcast_to(crossed, (8, *crossed.shape))
        return lax.all_to_all(copies, "z", 0, 0, axis_index_groups=[list(PLACE)], tiled=True)

    mine, theirs = known(kernels, rates_hist, core, 1)
    place, (partial_value, tiles) = after((mine + other_core(theirs), kernels))

    own_1 = kernels[0]
    far_1 = other_half(tiles[0])
    inner = other_core(tiles)
    diag_1 = other_core(far_1)
    both_gain = jnp.concatenate([gain, other_half(gain)])
    known_list = {2: known_halves(place, 2)}

    traction = summed(partial_value) + load_at(where, 1)
    traction_list = [traction]
    rate = jnp.tanh(gain * traction).astype(jnp.bfloat16)
    keep, send = halves(rate, 0, yl)
    place, crossed = after(spread(jnp.concatenate([keep, other_half(send)], axis=1)))
    known_list[3] = known_halves(place, 3)

    joined_list = []
    rates_last = None
    for moment in range(2, moments + 1):
        place, joined = after(joined_from(crossed))
        joined_list.append(joined)
        core_now, yl_now = place[0], place[1]
        keep, send = known_list[moment]
        got = other_half(send)
        one, two = tiles_first(joined, core_now == yl_now)
        near = times(one, own_1) + times(two, inner[0])
        far = times(one, far_1) + times(two, diag_1)
        partial_value = jnp.concatenate(
            [keep + near.reshape(keep.shape), got + far.reshape(got.shape)], axis=-1
        )
        place, (partial_value, joined, one, two) = after((partial_value, joined, one, two))
        if moment == 2:
            known_list[4] = known_halves(place, 4)
        if moment < moments:
            place, wide = after(other_half(joined))
            far_one, far_two = tiles_first(wide, place[0] != place[1])
            for later in range(moment + 1, moments + 1):
                back = later - moment + 1
                keep, send = known_list[later]
                more = times(one, kernels[back - 1]) + times(two, inner[back - 1])
                keep = keep + more.reshape(keep.shape)
                more = times(far_one, kernels[back - 1]) + times(far_two, inner[back - 1])
                send = send + more.reshape(send.shape)
                known_list[later] = lax.optimization_barrier((keep, send))
        place, block = after(summed(partial_value))
        traction = in_order(block[:, :rows], other_half(block[:, rows:]), place[1] == 1)
        traction_list.append(traction)
        if moment < moments:
            crossed = spread(jnp.tanh(both_gain * block).astype(jnp.bfloat16))
        else:
            rate = jnp.tanh(gain * traction).astype(jnp.bfloat16)
            rates_last = moved(rate, lambda z, yl, u, k: (u, k, z, yl))

    own_share = jnp.stack(
        [lax.dynamic_index_in_dim(joined, plane, 0, keepdims=False) for joined in joined_list]
    )
    crossed = [
        moved(
            own_share[..., rows * j : rows * (j + 1)],
            lambda z, yl, u, k, j=j: (z, k, u, yl ^ j),
        )
        for j in range(2)
    ]
    early = in_order(crossed[0], crossed[1], core == 1)
    rates = jnp.concatenate([early, rates_last[None]], axis=0)
    tractions = jnp.stack(traction_list)
    return jnp.swapaxes(rates, 1, 2), jnp.swapaxes(tractions, 1, 2)


def solution(mesh):
    finer = Mesh(mesh.devices.reshape(SIZES), AXES)
    return jax.shard_map(
        per_device,
        mesh=finer,
        in_specs=(P(None, ROW, COL), P(None, ROW, None), P(None, COL, None), P(ROW)),
        out_specs=(P(None, COL, ROW), P(None, ROW, COL)),
        check_vma=False,
    )
```

```python
import jax
import jax.numpy as jnp
from jax import lax
from jax.experimental import pallas as pl
from jax.experimental.pallas import tpu as pltpu
from jax.sharding import Mesh
from jax.sharding import PartitionSpec as P

AXES = ("z", "yl", "x", "yh", "k")
SIZES = (8, 2, 4, 2, 2)
ROW = ("z", "yl")
CHIP = ("x", "yh")
COL = ("x", "yh", "k")
PLACE = tuple((u + 4) % 8 for u in range(8))


def pairs_of(move):
    def number(place):
        total = 0
        for size, at in zip(SIZES, place):
            total = total * size + at
        return total

    found = []
    for z in range(8):
        for yl in range(2):
            for u in range(8):
                for k in range(2):
                    to_z, to_yl, to_u, to_k = move(z, yl, u, k)
                    source = (z, yl, u // 2, u % 2, k)
                    target = (to_z, to_yl, to_u // 2, to_u % 2, to_k)
                    found.append((number(source), number(target)))
    return found


def moved(array, move):
    return lax.ppermute(array, AXES, pairs_of(move))


def other_core(array):
    return moved(array, lambda z, yl, u, k: (z, yl, u, 1 - k))


def known_kernel(core_ref, kernel_ref, rates_ref, mine_ref, theirs_ref, total, turned):
    step = pl.program_id(0)
    product = jnp.dot(kernel_ref[0], rates_ref[0], preferred_element_type=jnp.float32)

    @pl.when(step == 0)
    def _():
        total[...] = product

    @pl.when(step > 0)
    def _():
        total[...] += product

    @pl.when(step == pl.num_programs(0) - 1)
    def _():
        turned[...] = total[...].T
        core = core_ref[0]
        share = mine_ref.shape[1]
        for u in range(mine_ref.shape[0]):
            start = pl.multiple_of((2 * u + core) * share, share)
            mine_ref[u] = turned[pl.ds(start, share), :]
            start = pl.multiple_of((2 * u + 1 - core) * share, share)
            theirs_ref[u] = turned[pl.ds(start, share), :]


def known(kernels, rates_hist, core, moment):
    history, rows, scen = rates_hist.shape
    share = scen // 16
    out = jax.ShapeDtypeStruct((8, share, rows), jnp.float32)
    return pl.pallas_call(
        known_kernel,
        grid_spec=pltpu.PrefetchScalarGridSpec(
            num_scalar_prefetch=1,
            grid=(history,),
            in_specs=[
                pl.BlockSpec((1, rows, rows), lambda q, c: (moment - 1 + q, 0, 0)),
                pl.BlockSpec((1, rows, scen), lambda q, c: (history - 1 - q, 0, 0)),
            ],
            out_specs=[
                pl.BlockSpec((8, share, rows), lambda q, c: (0, 0, 0)),
                pl.BlockSpec((8, share, rows), lambda q, c: (0, 0, 0)),
            ],
            scratch_shapes=[
                pltpu.VMEM((rows, scen), jnp.float32),
                pltpu.VMEM((scen, rows), jnp.float32),
            ],
        ),
        out_shape=[out, out],
        cost_estimate=pl.CostEstimate(
            flops=2 * history * rows * rows * scen,
            bytes_accessed=2 * history * rows * (rows + scen) + 4 * rows * scen,
            transcendentals=0,
        ),
        name="known",
    )(core.reshape(1).astype(jnp.int32), kernels, rates_hist)


def advance_kernel(core_ref, joined_ref, own_ref, inner_ref, *refs):
    bases, out_ref = refs[:-1], refs[-1]
    core = core_ref[0]
    count, _, share, rows = joined_ref.shape
    parts = (((1,), (1,)), ((), ()))
    near = joined_ref[:, core].reshape(count * share, rows)
    product = lax.dot_general(near, own_ref[0], parts, preferred_element_type=jnp.float32)
    far = joined_ref[:, 1 - core].reshape(count * share, rows)
    product += lax.dot_general(far, inner_ref[0], parts, preferred_element_type=jnp.float32)
    product = product.reshape(count, share, rows)
    for base in bases:
        product += base[...]
    out_ref[...] = product


def advance(joined, kernels, inner, back, bases, core):
    _, _, share, rows = joined.shape
    tile = pl.BlockSpec((1, rows, rows), lambda j, c: (back - 1, 0, 0))
    ordered = pl.BlockSpec((2, share, rows), lambda j, c: ((j + 2) % 4, 0, 0))
    return pl.pallas_call(
        advance_kernel,
        grid_spec=pltpu.PrefetchScalarGridSpec(
            num_scalar_prefetch=1,
            grid=(4,),
            in_specs=[
                pl.BlockSpec((2, 2, share, rows), lambda j, c: (j, 0, 0, 0)),
                tile,
                tile,
                *[ordered for _ in bases],
            ],
            out_specs=ordered,
        ),
        out_shape=jax.ShapeDtypeStruct((8, share, rows), jnp.float32),
        cost_estimate=pl.CostEstimate(
            flops=2 * 16 * share * rows * rows,
            bytes_accessed=4 * rows * rows + (32 + 32 * (1 + len(bases))) * share * rows,
            transcendentals=0,
        ),
        name="advance",
    )(core.reshape(1).astype(jnp.int32), joined, kernels, inner, *bases)


def per_device(kernels, prestress, rates_hist, gain):
    moments, rows, scen = prestress.shape
    share = scen // 16
    core = lax.axis_index("k")
    yl = lax.axis_index("yl")
    plane = lax.axis_index("z")
    my_col = lax.axis_index(COL)

    def after(value):
        return lax.optimization_barrier(((core, my_col), value))

    def known_pair(place, moment):
        mine, theirs = known(kernels, rates_hist, place[0], moment)
        return [mine, other_core(theirs)]

    mine, theirs = known(kernels, rates_hist, core, 1)
    place, (partial_value, tiles) = after((mine + other_core(theirs), kernels))
    load = lax.dynamic_slice_in_dim(prestress, place[1] * share, share, 2)
    load = jnp.swapaxes(load, 1, 2)
    known_list = {2: known_pair(place, 2)}
    inner = other_core(tiles)

    joined_list = []
    traction_list = []
    for moment in range(1, moments + 1):
        arrived = lax.all_to_all(partial_value, CHIP, 0, 0, tiled=True)
        traction = arrived.sum(axis=0) + load[moment - 1]
        traction_list.append(traction)
        rate = jnp.tanh(gain * traction).astype(jnp.bfloat16)
        if moment == moments:
            break
        crossed = moved(rate, lambda z, yl, u, k: (PLACE[u], yl, z, k))
        place, crossed = after(crossed)
        copies = jnp.broadcast_to(crossed, (16, *crossed.shape))
        joined = lax.all_to_all(copies, ROW, 0, 0, tiled=True).reshape(8, 2, share, rows)
        joined_list.append(joined)
        if moment + 2 <= moments:
            known_list[moment + 2] = known_pair(place, moment + 2)
        for back in range(2, moment + 1):
            earlier = joined_list[moment - back]
            known_list[moment + 1] = [
                advance(earlier, kernels, inner, back, known_list[moment + 1], place[0])
            ]
        partial_value = advance(joined, kernels, inner, 1, known_list[moment + 1], core)

    last_rates = moved(rate, lambda z, yl, u, k: (u, k, z, yl))
    at = (plane + 4) % 8
    held = jnp.stack(
        [lax.dynamic_index_in_dim(joined, at, 0, keepdims=False) for joined in joined_list]
    )
    keep = lax.dynamic_index_in_dim(held, core, 1, keepdims=False)
    send = lax.dynamic_index_in_dim(held, 1 - core, 1, keepdims=False)
    early = jnp.where(yl == core, keep, other_core(send))
    rates = jnp.concatenate([early, last_rates[None]], axis=0)
    tractions = jnp.stack(traction_list)
    return jnp.swapaxes(rates, 1, 2), jnp.swapaxes(tractions, 1, 2)


def solution(mesh):
    finer = Mesh(mesh.devices.reshape(SIZES), AXES)
    return jax.shard_map(
        per_device,
        mesh=finer,
        in_specs=(P(None, ROW, COL), P(None, ROW, None), P(None, COL, None), P(ROW)),
        out_specs=(P(None, COL, ROW), P(None, ROW, COL)),
        check_vma=False,
    )
```

```python
import jax
import jax.numpy as jnp
import numpy as np
from jax import lax
from jax.experimental import pallas as pl
from jax.experimental.pallas import tpu as pltpu
from jax.sharding import Mesh
from jax.sharding import PartitionSpec as P

AXES = ("z", "yl", "x", "yh", "k")
SIZES = (8, 2, 4, 2, 2)
ROW = ("z", "yl")
CHIP = ("x", "yh")
COL = ("x", "yh", "k")
STEP = {(2, 1): 0, (1, 1): 1, (3, 1): -1, (2, 0): 2, (0, 1): -2, (1, 0): 3, (3, 0): -3, (0, 0): 4}


def place_of(u, m):
    return (m + STEP[(u // 2 - m // 2) % 4, (u - m) % 2]) % 8


PLACES = np.array([[place_of(u, m) for u in range(8)] for m in range(8)], np.int32)


def pairs_of(move):
    def number(place):
        total = 0
        for size, at in zip(SIZES, place):
            total = total * size + at
        return total

    found = []
    for z in range(8):
        for yl in range(2):
            for u in range(8):
                for k in range(2):
                    to_z, to_yl, to_u, to_k = move(z, yl, u, k)
                    source = (z, yl, u // 2, u % 2, k)
                    target = (to_z, to_yl, to_u // 2, to_u % 2, to_k)
                    found.append((number(source), number(target)))
    return found


def moved(array, move):
    return lax.ppermute(array, AXES, pairs_of(move))


def other_core(array):
    return moved(array, lambda z, yl, u, k: (z, yl, u, 1 - k))


def known_kernel(place_ref, kernel_ref, rates_ref, mine_ref, theirs_ref, total, turned):
    step = pl.program_id(0)
    product = jnp.dot(kernel_ref[0], rates_ref[0], preferred_element_type=jnp.float32)

    @pl.when(step == 0)
    def _():
        total[...] = product

    @pl.when(step > 0)
    def _():
        total[...] += product

    @pl.when(step == pl.num_programs(0) - 1)
    def _():
        turned[...] = total[...].T
        core = place_ref[0]
        share = mine_ref.shape[1]
        for u in range(mine_ref.shape[0]):
            start = pl.multiple_of((2 * u + core) * share, share)
            mine_ref[u] = turned[pl.ds(start, share), :]
            start = pl.multiple_of((2 * u + 1 - core) * share, share)
            theirs_ref[u] = turned[pl.ds(start, share), :]


def known(kernels, rates_hist, place, moment):
    history, rows, scen = rates_hist.shape
    share = scen // 16
    out = jax.ShapeDtypeStruct((8, share, rows), jnp.float32)
    return pl.pallas_call(
        known_kernel,
        grid_spec=pltpu.PrefetchScalarGridSpec(
            num_scalar_prefetch=1,
            grid=(history,),
            in_specs=[
                pl.BlockSpec((1, rows, rows), lambda q, c: (moment - 1 + q, 0, 0)),
                pl.BlockSpec((1, rows, scen), lambda q, c: (history - 1 - q, 0, 0)),
            ],
            out_specs=[
                pl.BlockSpec((8, share, rows), lambda q, c: (0, 0, 0)),
                pl.BlockSpec((8, share, rows), lambda q, c: (0, 0, 0)),
            ],
            scratch_shapes=[
                pltpu.VMEM((rows, scen), jnp.float32),
                pltpu.VMEM((scen, rows), jnp.float32),
            ],
        ),
        out_shape=[out, out],
        cost_estimate=pl.CostEstimate(
            flops=2 * history * rows * rows * scen,
            bytes_accessed=2 * history * rows * (rows + scen) + 4 * rows * scen,
            transcendentals=0,
        ),
        name="known",
    )(place, kernels, rates_hist)


def advance_kernel(place_ref, joined_ref, own_ref, inner_ref, *refs):
    bases, out_ref, near, far = refs[:-3], refs[-3], refs[-2], refs[-1]
    core = place_ref[0]
    count, share, rows = out_ref.shape
    for u in range(count):
        at = place_ref[1 + u]
        near[u] = joined_ref[at, core]
        far[u] = joined_ref[at, 1 - core]
    parts = (((1,), (1,)), ((), ()))
    product = lax.dot_general(
        near[...].reshape(count * share, rows), own_ref[0], parts, preferred_element_type=jnp.float32
    )
    product += lax.dot_general(
        far[...].reshape(count * share, rows), inner_ref[0], parts, preferred_element_type=jnp.float32
    )
    product = product.reshape(count, share, rows)
    for base in bases:
        product += base[...]
    out_ref[...] = product


def advance(joined, kernels, inner, back, bases, place):
    _, _, share, rows = joined.shape
    tile = pl.BlockSpec((1, rows, rows), lambda j, c: (back - 1, 0, 0))
    whole = pl.BlockSpec((8, share, rows), lambda j, c: (0, 0, 0))
    return pl.pallas_call(
        advance_kernel,
        grid_spec=pltpu.PrefetchScalarGridSpec(
            num_scalar_prefetch=1,
            grid=(1,),
            in_specs=[
                pl.BlockSpec((8, 2, share, rows), lambda j, c: (0, 0, 0, 0)),
                tile,
                tile,
                *[whole for _ in bases],
            ],
            out_specs=whole,
            scratch_shapes=[
                pltpu.VMEM((8, share, rows), jnp.bfloat16),
                pltpu.VMEM((8, share, rows), jnp.bfloat16),
            ],
        ),
        out_shape=jax.ShapeDtypeStruct((8, share, rows), jnp.float32),
        cost_estimate=pl.CostEstimate(
            flops=2 * 16 * share * rows * rows,
            bytes_accessed=4 * rows * rows + (32 + 32 * (1 + len(bases))) * share * rows,
            transcendentals=0,
        ),
        name="advance",
    )(place, joined, kernels, inner, *bases)


def per_device(kernels, prestress, rates_hist, gain):
    moments, rows, scen = prestress.shape
    share = scen // 16
    core = lax.axis_index("k")
    yl = lax.axis_index("yl")
    plane = lax.axis_index("z")
    chip = lax.axis_index(CHIP)
    my_col = lax.axis_index(COL)
    order = lax.dynamic_index_in_dim(jnp.asarray(PLACES), chip, 0, keepdims=False)
    place = jnp.concatenate([core.reshape(1).astype(jnp.int32), order])

    def after(value):
        return lax.optimization_barrier((place, value))

    def known_at(place, moment):
        return known(kernels, rates_hist, place, moment)

    def reduced(partial_value, moment, beside):
        arrived = lax.all_to_all(partial_value, CHIP, 0, 0, tiled=True)
        _, (arrived, beside) = after((arrived, beside))
        traction = arrived.sum(axis=0) + load[moment - 1]
        return traction, jnp.tanh(gain * traction).astype(jnp.bfloat16), beside

    def crossing(rate):
        return moved(rate, lambda z, yl, u, k: (place_of(u, z), yl, z, k))

    def joining(crossed):
        copies = jnp.broadcast_to(crossed, (16, *crossed.shape))
        return lax.all_to_all(copies, ROW, 0, 0, tiled=True).reshape(8, 2, share, rows)

    mine, theirs = known_at(place, 1)
    now, (partial_value, tiles) = after((mine + other_core(theirs), kernels))
    load = lax.dynamic_slice_in_dim(prestress, my_col * share, share, 2)
    load = jnp.swapaxes(load, 1, 2)
    inner = other_core(tiles)

    known_2 = known_at(now, 2)
    traction_1, rate, known_2 = reduced(partial_value, 1, known_2)
    now, crossed = after(crossing(rate))
    mine_2, theirs_2 = known_2[0], other_core(known_2[1])
    known_3 = known_at(now, 3)
    joined_1 = joining(crossed)
    partial_value = advance(joined_1, kernels, inner, 1, [mine_2, theirs_2], place)

    now, (partial_value, known_3) = after((partial_value, known_3))
    mine_3, theirs_3 = known_3[0], other_core(known_3[1])
    known_3 = advance(joined_1, kernels, inner, 2, [mine_3, theirs_3], now)
    traction_2, rate, known_3 = reduced(partial_value, 2, known_3)
    now, crossed = after(crossing(rate))
    known_4 = known_at(now, 4)
    from_1 = advance(joined_1, kernels, inner, 3, [], now)
    joined_2 = joining(crossed)
    partial_value = advance(joined_2, kernels, inner, 1, [known_3], place)

    now, (partial_value, known_4, from_1) = after((partial_value, known_4, from_1))
    mine_4, theirs_4 = known_4[0], other_core(known_4[1])
    traction_3, rate, _ = reduced(partial_value, 3, [])
    now, crossed = after(crossing(rate))
    known_4 = advance(joined_2, kernels, inner, 2, [mine_4, theirs_4, from_1], now)
    joined_3 = joining(crossed)
    partial_value = advance(joined_3, kernels, inner, 1, [known_4], place)

    now, (partial_value, joined_list) = after((partial_value, [joined_1, joined_2, joined_3]))
    traction_4, rate, _ = reduced(partial_value, 4, [])
    last_rates = moved(rate, lambda z, yl, u, k: (u, k, z, yl))
    at = lax.dynamic_index_in_dim(now, 1 + plane, 0, keepdims=False)
    held = jnp.stack(
        [lax.dynamic_index_in_dim(joined, at, 0, keepdims=False) for joined in joined_list]
    )
    keep = lax.dynamic_index_in_dim(held, core, 1, keepdims=False)
    send = lax.dynamic_index_in_dim(held, 1 - core, 1, keepdims=False)
    early = jnp.where(yl == core, keep, other_core(send))
    rates = jnp.concatenate([early, last_rates[None]], axis=0)
    tractions = jnp.stack([traction_1, traction_2, traction_3, traction_4])
    return jnp.swapaxes(rates, 1, 2), jnp.swapaxes(tractions, 1, 2)


def solution(mesh):
    finer = Mesh(mesh.devices.reshape(SIZES), AXES)
    return jax.shard_map(
        per_device,
        mesh=finer,
        in_specs=(P(None, ROW, COL), P(None, ROW, None), P(None, COL, None), P(ROW)),
        out_specs=(P(None, COL, ROW), P(None, ROW, COL)),
        check_vma=False,
    )
```

```python
import jax
import jax.numpy as jnp
import numpy as np
from jax import lax
from jax.experimental import pallas as pl
from jax.experimental.pallas import tpu as pltpu
from jax.sharding import Mesh
from jax.sharding import PartitionSpec as P

AXES = ("z", "yl", "x", "yh", "k")
SIZES = (8, 2, 4, 2, 2)
ROW = ("z", "yl")
CHIP = ("x", "yh")
COL = ("x", "yh", "k")
STEP = {(2, 1): 0, (1, 1): 1, (3, 1): -1, (2, 0): 2, (0, 1): -2, (1, 0): 3, (3, 0): -3, (0, 0): 4}


def place_of(u, m):
    return (m + STEP[(u // 2 - m // 2) % 4, (u - m) % 2]) % 8


PLACES = np.array([[place_of(u, m) for u in range(8)] for m in range(8)], np.int32)

GRANT = 20 * 2**20


def pairs_of(move):
    def number(place):
        total = 0
        for size, at in zip(SIZES, place):
            total = total * size + at
        return total

    found = []
    for z in range(8):
        for yl in range(2):
            for u in range(8):
                for k in range(2):
                    to_z, to_yl, to_u, to_k = move(z, yl, u, k)
                    source = (z, yl, u // 2, u % 2, k)
                    target = (to_z, to_yl, to_u // 2, to_u % 2, to_k)
                    found.append((number(source), number(target)))
    return found


def moved(array, move):
    return lax.ppermute(array, AXES, pairs_of(move))


def other_core(array):
    return moved(array, lambda z, yl, u, k: (z, yl, u, 1 - k))


def in_hbm(array):
    return pltpu.with_memory_space_constraint(array, pltpu.HBM)


def known_kernel(kernel_ref, rates_ref, mine_ref, theirs_ref, total, turned):
    step = pl.program_id(0)
    product = jnp.dot(kernel_ref[0], rates_ref[0], preferred_element_type=jnp.float32)

    @pl.when(step == 0)
    def _():
        total[...] = product

    @pl.when(step > 0)
    def _():
        total[...] += product

    @pl.when(step == pl.num_programs(0) - 1)
    def _():
        turned[...] = total[...].T
        core = lax.axis_index("k")
        share = mine_ref.shape[1]
        for u in range(mine_ref.shape[0]):
            start = pl.multiple_of((2 * u + core) * share, share)
            mine_ref[u] = turned[pl.ds(start, share), :]
            start = pl.multiple_of((2 * u + 1 - core) * share, share)
            theirs_ref[u] = turned[pl.ds(start, share), :]


def known(kernels, rates_hist, moment):
    history, rows, scen = rates_hist.shape
    share = scen // 16
    out = jax.ShapeDtypeStruct((8, share, rows), jnp.float32)
    return pl.pallas_call(
        known_kernel,
        grid=(history,),
        in_specs=[
            pl.BlockSpec((1, rows, rows), lambda q: (moment - 1 + q, 0, 0)),
            pl.BlockSpec((1, rows, scen), lambda q: (history - 1 - q, 0, 0)),
        ],
        out_specs=[
            pl.BlockSpec((8, share, rows), lambda q: (0, 0, 0)),
            pl.BlockSpec((8, share, rows), lambda q: (0, 0, 0)),
        ],
        scratch_shapes=[
            pltpu.VMEM((rows, scen), jnp.float32),
            pltpu.VMEM((scen, rows), jnp.float32),
        ],
        out_shape=[out, out],
        compiler_params=pltpu.CompilerParams(vmem_limit_bytes=GRANT),
        cost_estimate=pl.CostEstimate(
            flops=2 * history * rows * rows * scen,
            bytes_accessed=2 * history * rows * (rows + scen) + 4 * rows * scen,
            transcendentals=0,
        ),
        name="known",
    )(in_hbm(kernels), in_hbm(rates_hist))


def advance_kernel(place_ref, joined_ref, own_ref, inner_ref, *refs):
    bases, out_ref, near, far = refs[:-3], refs[-3], refs[-2], refs[-1]
    core = place_ref[0]
    count, share, rows = out_ref.shape
    for u in range(count):
        at = place_ref[1 + u]
        near[u] = joined_ref[at, core]
        far[u] = joined_ref[at, 1 - core]
    parts = (((1,), (1,)), ((), ()))
    product = lax.dot_general(
        near[...].reshape(count * share, rows), own_ref[0], parts, preferred_element_type=jnp.float32
    )
    product += lax.dot_general(
        far[...].reshape(count * share, rows), inner_ref[0], parts, preferred_element_type=jnp.float32
    )
    product = product.reshape(count, share, rows)
    for base in bases:
        product += base[...]
    out_ref[...] = product


def advance(joined, kernels, inner, back, bases, place):
    _, _, share, rows = joined.shape
    tile = pl.BlockSpec((1, rows, rows), lambda j, c: (back - 1, 0, 0))
    whole = pl.BlockSpec((8, share, rows), lambda j, c: (0, 0, 0))
    return pl.pallas_call(
        advance_kernel,
        grid_spec=pltpu.PrefetchScalarGridSpec(
            num_scalar_prefetch=1,
            grid=(1,),
            in_specs=[
                pl.BlockSpec((8, 2, share, rows), lambda j, c: (0, 0, 0, 0)),
                tile,
                tile,
                *[whole for _ in bases],
            ],
            out_specs=whole,
            scratch_shapes=[
                pltpu.VMEM((8, share, rows), jnp.bfloat16),
                pltpu.VMEM((8, share, rows), jnp.bfloat16),
            ],
        ),
        out_shape=jax.ShapeDtypeStruct((8, share, rows), jnp.float32),
        compiler_params=pltpu.CompilerParams(vmem_limit_bytes=GRANT),
        cost_estimate=pl.CostEstimate(
            flops=2 * 16 * share * rows * rows,
            bytes_accessed=4 * rows * rows + (32 + 32 * (1 + len(bases))) * share * rows,
            transcendentals=0,
        ),
        name="advance",
    )(place, joined, in_hbm(kernels), in_hbm(inner), *map(in_hbm, bases))


def per_device(kernels, prestress, rates_hist, gain):
    moments, rows, scen = prestress.shape
    share = scen // 16
    core = lax.axis_index("k")
    yl = lax.axis_index("yl")
    plane = lax.axis_index("z")
    chip = lax.axis_index(CHIP)
    my_col = lax.axis_index(COL)
    order = lax.dynamic_index_in_dim(jnp.asarray(PLACES), chip, 0, keepdims=False)
    place = jnp.concatenate([core.reshape(1).astype(jnp.int32), order])

    def after(value):
        return lax.optimization_barrier((place, value))

    def reduced(partial_value, moment, beside):
        arrived = lax.all_to_all(partial_value, CHIP, 0, 0, tiled=True)
        _, (arrived, beside) = after((arrived, beside))
        traction = arrived.sum(axis=0) + load[moment - 1]
        return traction, jnp.tanh(gain * traction).astype(jnp.bfloat16), beside

    def crossing(rate):
        return moved(rate, lambda z, yl, u, k: (place_of(u, z), yl, z, k))

    def joining(crossed):
        copies = jnp.broadcast_to(crossed, (16, *crossed.shape))
        return lax.all_to_all(copies, ROW, 0, 0, tiled=True).reshape(8, 2, share, rows)

    mine, theirs = known(kernels, rates_hist, 1)
    now, (partial_value, tiles, hist) = after((mine + other_core(theirs), kernels, rates_hist))
    load = lax.dynamic_slice_in_dim(prestress, my_col * share, share, 2)
    load = jnp.swapaxes(load, 1, 2)
    inner = other_core(tiles)

    known_2 = known(tiles, hist, 2)
    traction_1, rate, known_2 = reduced(partial_value, 1, known_2)
    now, (crossed, tiles, hist) = after((crossing(rate), kernels, rates_hist))
    mine_2, theirs_2 = known_2[0], other_core(known_2[1])
    known_3 = known(tiles, hist, 3)
    known_3 = [known_3[0], other_core(known_3[1])]
    joined_1 = joining(crossed)
    partial_value = advance(joined_1, kernels, inner, 1, [mine_2, theirs_2], place)

    now, (partial_value, known_3) = after((partial_value, known_3))
    known_3 = advance(joined_1, kernels, inner, 2, known_3, now)
    traction_2, rate, known_3 = reduced(partial_value, 2, known_3)
    now, (crossed, tiles, hist) = after((crossing(rate), kernels, rates_hist))
    known_4 = known(tiles, hist, 4)
    known_4 = [known_4[0], other_core(known_4[1])]
    from_1 = advance(joined_1, kernels, inner, 3, [], now)
    joined_2 = joining(crossed)
    partial_value = advance(joined_2, kernels, inner, 1, [known_3], place)

    now, (partial_value, known_4, from_1) = after((partial_value, known_4, from_1))
    traction_3, rate, _ = reduced(partial_value, 3, [])
    now, crossed = after(crossing(rate))
    at = lax.dynamic_index_in_dim(now, 1 + plane, 0, keepdims=False)
    known_4 = advance(joined_2, kernels, inner, 2, [*known_4, from_1], now)
    joined_3 = joining(crossed)
    partial_value = advance(joined_3, kernels, inner, 1, [known_4], place)

    _, (partial_value, joined_list) = after((partial_value, [joined_1, joined_2, joined_3]))
    traction_4, rate, _ = reduced(partial_value, 4, [])
    last_rates = moved(rate, lambda z, yl, u, k: (u, k, z, yl))
    held = jnp.stack(
        [lax.dynamic_index_in_dim(joined, at, 0, keepdims=False) for joined in joined_list]
    )
    keep = lax.dynamic_index_in_dim(held, core, 1, keepdims=False)
    send = lax.dynamic_index_in_dim(held, 1 - core, 1, keepdims=False)
    early = jnp.where(yl == core, keep, other_core(send))
    rates = jnp.concatenate([early, last_rates[None]], axis=0)
    tractions = jnp.stack([traction_1, traction_2, traction_3, traction_4])
    return jnp.swapaxes(rates, 1, 2), jnp.swapaxes(tractions, 1, 2)


def solution(mesh):
    finer = Mesh(mesh.devices.reshape(SIZES), AXES)
    return jax.shard_map(
        per_device,
        mesh=finer,
        in_specs=(P(None, ROW, COL), P(None, ROW, None), P(None, COL, None), P(ROW)),
        out_specs=(P(None, COL, ROW), P(None, ROW, COL)),
        check_vma=False,
    )
```

```python
import jax
import jax.numpy as jnp
import numpy as np
from jax import lax
from jax.experimental import pallas as pl
from jax.experimental.pallas import tpu as pltpu
from jax.sharding import Mesh
from jax.sharding import PartitionSpec as P

AXES = ("z", "yl", "x", "yh", "k")
SIZES = (8, 2, 4, 2, 2)
ROW = ("z", "yl")
CHIP = ("x", "yh")
COL = ("x", "yh", "k")
STEP = {(2, 1): 0, (1, 1): 1, (3, 1): -1, (2, 0): 2, (0, 1): -2, (1, 0): 3, (3, 0): -3, (0, 0): 4}


def place_of(u, m):
    return (m + STEP[(u // 2 - m // 2) % 4, (u - m) % 2]) % 8


PLACES = np.array([[place_of(u, m) for u in range(8)] for m in range(8)], np.int32)

GRANT = 20 * 2**20


def pairs_of(move):
    def number(place):
        total = 0
        for size, at in zip(SIZES, place):
            total = total * size + at
        return total

    found = []
    for z in range(8):
        for yl in range(2):
            for u in range(8):
                for k in range(2):
                    to_z, to_yl, to_u, to_k = move(z, yl, u, k)
                    source = (z, yl, u // 2, u % 2, k)
                    target = (to_z, to_yl, to_u // 2, to_u % 2, to_k)
                    found.append((number(source), number(target)))
    return found


def moved(array, move):
    return lax.ppermute(array, AXES, pairs_of(move))


def other_core(array):
    return moved(array, lambda z, yl, u, k: (z, yl, u, 1 - k))


def in_hbm(array):
    return pltpu.with_memory_space_constraint(array, pltpu.HBM)


def known_kernel(kernel_ref, rates_ref, mine_ref, theirs_ref, total, turned):
    step = pl.program_id(0)
    product = jnp.dot(kernel_ref[0], rates_ref[0], preferred_element_type=jnp.float32)

    @pl.when(step == 0)
    def _():
        total[...] = product

    @pl.when(step > 0)
    def _():
        total[...] += product

    @pl.when(step == pl.num_programs(0) - 1)
    def _():
        turned[...] = total[...].T
        core = lax.axis_index("k")
        share = mine_ref.shape[1]
        for u in range(mine_ref.shape[0]):
            start = pl.multiple_of((2 * u + core) * share, share)
            mine_ref[u] = turned[pl.ds(start, share), :]
            start = pl.multiple_of((2 * u + 1 - core) * share, share)
            theirs_ref[u] = turned[pl.ds(start, share), :]


def known(kernels, rates_hist, moment):
    history, rows, scen = rates_hist.shape
    share = scen // 16
    shape = (8, share, rows)
    if moment == 1:
        out = jax.ShapeDtypeStruct(shape, jnp.float32)
    else:
        out = pltpu.HBM(shape, jnp.float32)
    return pl.pallas_call(
        known_kernel,
        grid=(history,),
        in_specs=[
            pl.BlockSpec((1, rows, rows), lambda q: (moment - 1 + q, 0, 0)),
            pl.BlockSpec((1, rows, scen), lambda q: (history - 1 - q, 0, 0)),
        ],
        out_specs=[
            pl.BlockSpec((8, share, rows), lambda q: (0, 0, 0)),
            pl.BlockSpec((8, share, rows), lambda q: (0, 0, 0)),
        ],
        scratch_shapes=[
            pltpu.VMEM((rows, scen), jnp.float32),
            pltpu.VMEM((scen, rows), jnp.float32),
        ],
        out_shape=[out, out],
        compiler_params=pltpu.CompilerParams(vmem_limit_bytes=GRANT),
        cost_estimate=pl.CostEstimate(
            flops=2 * history * rows * rows * scen,
            bytes_accessed=2 * history * rows * (rows + scen) + 4 * rows * scen,
            transcendentals=0,
        ),
        name="known",
    )(in_hbm(kernels), in_hbm(rates_hist))


def advance_kernel(place_ref, joined_ref, own_ref, inner_ref, *refs):
    bases, out_ref, near, far = refs[:-3], refs[-3], refs[-2], refs[-1]
    core = place_ref[0]
    count, share, rows = near.shape

    @pl.when(pl.program_id(0) == 0)
    def _():
        for u in range(count):
            at = place_ref[1 + u]
            near[u] = joined_ref[at, core]
            far[u] = joined_ref[at, 1 - core]

    parts = (((1,), (1,)), ((), ()))
    product = lax.dot_general(
        near[...].reshape(count * share, rows), own_ref[0], parts, preferred_element_type=jnp.float32
    )
    product += lax.dot_general(
        far[...].reshape(count * share, rows), inner_ref[0], parts, preferred_element_type=jnp.float32
    )
    product = product.reshape(out_ref.shape)
    for base in bases:
        product += base[...]
    out_ref[...] = product


def advance(joined, kernels, inner, back, bases, place):
    _, _, share, rows = joined.shape
    block = rows // 2
    tile = pl.BlockSpec((1, block, rows), lambda j, c: (back - 1, j, 0))
    whole = pl.BlockSpec((8, share, block), lambda j, c: (0, 0, j))
    return pl.pallas_call(
        advance_kernel,
        grid_spec=pltpu.PrefetchScalarGridSpec(
            num_scalar_prefetch=1,
            grid=(2,),
            in_specs=[
                pl.BlockSpec((8, 2, share, rows), lambda j, c: (0, 0, 0, 0)),
                tile,
                tile,
                *[whole for _ in bases],
            ],
            out_specs=whole,
            scratch_shapes=[
                pltpu.VMEM((8, share, rows), jnp.bfloat16),
                pltpu.VMEM((8, share, rows), jnp.bfloat16),
            ],
        ),
        out_shape=pltpu.HBM((8, share, rows), jnp.float32),
        compiler_params=pltpu.CompilerParams(vmem_limit_bytes=GRANT),
        cost_estimate=pl.CostEstimate(
            flops=2 * 16 * share * rows * rows,
            bytes_accessed=4 * rows * rows + (32 + 32 * (1 + len(bases))) * share * rows,
            transcendentals=0,
        ),
        name="advance",
    )(place, joined, in_hbm(kernels), in_hbm(inner), *map(in_hbm, bases))


def per_device(kernels, prestress, rates_hist, gain):
    moments, rows, scen = prestress.shape
    share = scen // 16
    core = lax.axis_index("k")
    yl = lax.axis_index("yl")
    plane = lax.axis_index("z")
    chip = lax.axis_index(CHIP)
    my_col = lax.axis_index(COL)
    order = lax.dynamic_index_in_dim(jnp.asarray(PLACES), chip, 0, keepdims=False)
    place = jnp.concatenate([core.reshape(1).astype(jnp.int32), order])

    def after(value):
        return lax.optimization_barrier((place, value))

    def reduced(partial_value, moment, beside):
        arrived = lax.all_to_all(partial_value, CHIP, 0, 0, tiled=True)
        _, (arrived, beside) = after((arrived, beside))
        traction = arrived.sum(axis=0) + load[moment - 1]
        return traction, jnp.tanh(gain * traction).astype(jnp.bfloat16), beside

    def crossing(rate):
        return moved(rate, lambda z, yl, u, k: (place_of(u, z), yl, z, k))

    def joining(crossed):
        copies = jnp.broadcast_to(crossed, (16, *crossed.shape))
        return lax.all_to_all(copies, ROW, 0, 0, tiled=True).reshape(8, 2, share, rows)

    mine, theirs = known(kernels, rates_hist, 1)
    now, (partial_value, tiles, hist) = after((mine + other_core(theirs), kernels, rates_hist))
    load = lax.dynamic_slice_in_dim(prestress, my_col * share, share, 2)
    load = jnp.swapaxes(load, 1, 2)
    inner = other_core(tiles)

    known_2 = known(tiles, hist, 2)
    traction_1, rate, known_2 = reduced(partial_value, 1, known_2)
    now, (crossed, tiles, hist, known_2) = after((crossing(rate), kernels, rates_hist, known_2))
    known_2 = known_2[0] + other_core(known_2[1])
    tiles, hist, known_2 = lax.optimization_barrier((tiles, hist, known_2))
    known_3 = known(tiles, hist, 3)
    known_3 = [known_3[0], other_core(known_3[1])]
    joined_1 = joining(crossed)
    partial_value = advance(joined_1, kernels, inner, 1, [known_2], place)

    now, (partial_value, known_3) = after((partial_value, known_3))
    known_3 = advance(joined_1, kernels, inner, 2, known_3, now)
    traction_2, rate, known_3 = reduced(partial_value, 2, known_3)
    now, (crossed, tiles, hist) = after((crossing(rate), kernels, rates_hist))
    known_4 = known(tiles, hist, 4)
    known_4 = [known_4[0], other_core(known_4[1])]
    from_1 = advance(joined_1, kernels, inner, 3, [], now)
    joined_2 = joining(crossed)
    partial_value = advance(joined_2, kernels, inner, 1, [known_3], place)

    now, (partial_value, known_4, from_1) = after((partial_value, known_4, from_1))
    traction_3, rate, _ = reduced(partial_value, 3, [])
    now, crossed = after(crossing(rate))
    at = lax.dynamic_index_in_dim(now, 1 + plane, 0, keepdims=False)
    known_4 = advance(joined_2, kernels, inner, 2, [*known_4, from_1], now)
    joined_3 = joining(crossed)
    partial_value = advance(joined_3, kernels, inner, 1, [known_4], place)

    _, (partial_value, joined_list) = after((partial_value, [joined_1, joined_2, joined_3]))
    traction_4, rate, _ = reduced(partial_value, 4, [])
    tractions = [traction_1, traction_2, traction_3, traction_4]
    rate, tractions = lax.optimization_barrier((rate, tractions))
    last_rates = moved(rate, lambda z, yl, u, k: (u, k, z, yl))
    held = jnp.stack(
        [lax.dynamic_index_in_dim(joined, at, 0, keepdims=False) for joined in joined_list]
    )
    keep = lax.dynamic_index_in_dim(held, core, 1, keepdims=False)
    send = lax.dynamic_index_in_dim(held, 1 - core, 1, keepdims=False)
    early = jnp.where(yl == core, keep, other_core(send))
    rates = jnp.concatenate([early, last_rates[None]], axis=0)
    tractions = jnp.stack(tractions)
    return jnp.swapaxes(rates, 1, 2), jnp.swapaxes(tractions, 1, 2)


def solution(mesh):
    finer = Mesh(mesh.devices.reshape(SIZES), AXES)
    return jax.shard_map(
        per_device,
        mesh=finer,
        in_specs=(P(None, ROW, COL), P(None, ROW, None), P(None, COL, None), P(ROW)),
        out_specs=(P(None, COL, ROW), P(None, ROW, COL)),
        check_vma=False,
    )
```

```python
import jax
import jax.numpy as jnp
import numpy as np
from jax import lax
from jax.experimental import pallas as pl
from jax.experimental.pallas import tpu as pltpu
from jax.sharding import Mesh
from jax.sharding import PartitionSpec as P

AXES = ("z", "yl", "x", "yh", "k")
SIZES = (8, 2, 4, 2, 2)
ROW = ("z", "yl")
CHIP = ("x", "yh")
COL = ("x", "yh", "k")
STEP = {(2, 1): 0, (1, 1): 1, (3, 1): -1, (2, 0): 2, (0, 1): -2, (1, 0): 3, (3, 0): -3, (0, 0): 4}


def place_of(u, m):
    return (m + STEP[(u // 2 - m // 2) % 4, (u - m) % 2]) % 8


PLACES = np.array([[place_of(u, m) for u in range(8)] for m in range(8)], np.int32)

GRANT = 20 * 2**20


def pairs_of(move):
    def number(place):
        total = 0
        for size, at in zip(SIZES, place):
            total = total * size + at
        return total

    found = []
    for z in range(8):
        for yl in range(2):
            for u in range(8):
                for k in range(2):
                    to_z, to_yl, to_u, to_k = move(z, yl, u, k)
                    source = (z, yl, u // 2, u % 2, k)
                    target = (to_z, to_yl, to_u // 2, to_u % 2, to_k)
                    found.append((number(source), number(target)))
    return found


def moved(array, move):
    return lax.ppermute(array, AXES, pairs_of(move))


def other_core(array):
    return moved(array, lambda z, yl, u, k: (z, yl, u, 1 - k))


def in_hbm(array):
    return pltpu.with_memory_space_constraint(array, pltpu.HBM)


def known_kernel(kernel_ref, rates_ref, mine_ref, theirs_ref, total, turned):
    step = pl.program_id(0)
    product = jnp.dot(kernel_ref[0], rates_ref[0], preferred_element_type=jnp.float32)

    @pl.when(step == 0)
    def _():
        total[...] = product

    @pl.when(step > 0)
    def _():
        total[...] += product

    @pl.when(step == pl.num_programs(0) - 1)
    def _():
        turned[...] = total[...].T
        core = lax.axis_index("k")
        share = mine_ref.shape[1]
        for u in range(mine_ref.shape[0]):
            start = pl.multiple_of((2 * u + core) * share, share)
            mine_ref[u] = turned[pl.ds(start, share), :]
            start = pl.multiple_of((2 * u + 1 - core) * share, share)
            theirs_ref[u] = turned[pl.ds(start, share), :]


def known(kernels, rates_hist, moment):
    history, rows, scen = rates_hist.shape
    share = scen // 16
    out = jax.ShapeDtypeStruct((8, share, rows), jnp.float32)
    return pl.pallas_call(
        known_kernel,
        grid=(history,),
        in_specs=[
            pl.BlockSpec((1, rows, rows), lambda q: (moment - 1 + q, 0, 0)),
            pl.BlockSpec((1, rows, scen), lambda q: (history - 1 - q, 0, 0)),
        ],
        out_specs=[
            pl.BlockSpec((8, share, rows), lambda q: (0, 0, 0)),
            pl.BlockSpec((8, share, rows), lambda q: (0, 0, 0)),
        ],
        scratch_shapes=[
            pltpu.VMEM((rows, scen), jnp.float32),
            pltpu.VMEM((scen, rows), jnp.float32),
        ],
        out_shape=[out, out],
        compiler_params=pltpu.CompilerParams(vmem_limit_bytes=GRANT),
        cost_estimate=pl.CostEstimate(
            flops=2 * history * rows * rows * scen,
            bytes_accessed=2 * history * rows * (rows + scen) + 4 * rows * scen,
            transcendentals=0,
        ),
        name="known",
    )(in_hbm(kernels), in_hbm(rates_hist))


def advance_kernel(place_ref, joined_ref, own_ref, inner_ref, *refs):
    bases, out_ref, near, far = refs[:-3], refs[-3], refs[-2], refs[-1]
    core = place_ref[0]
    count, share, rows = out_ref.shape
    for u in range(count):
        at = place_ref[1 + u]
        near[u] = joined_ref[at, core]
        far[u] = joined_ref[at, 1 - core]
    parts = (((1,), (1,)), ((), ()))
    product = lax.dot_general(
        near[...].reshape(count * share, rows), own_ref[0], parts, preferred_element_type=jnp.float32
    )
    product += lax.dot_general(
        far[...].reshape(count * share, rows), inner_ref[0], parts, preferred_element_type=jnp.float32
    )
    product = product.reshape(count, share, rows)
    for base in bases:
        product += base[...]
    out_ref[...] = product


def advance(joined, kernels, inner, back, bases, place):
    _, _, share, rows = joined.shape
    tile = pl.BlockSpec((1, rows, rows), lambda j, c: (back - 1, 0, 0))
    whole = pl.BlockSpec((8, share, rows), lambda j, c: (0, 0, 0))
    return pl.pallas_call(
        advance_kernel,
        grid_spec=pltpu.PrefetchScalarGridSpec(
            num_scalar_prefetch=1,
            grid=(1,),
            in_specs=[
                pl.BlockSpec((8, 2, share, rows), lambda j, c: (0, 0, 0, 0)),
                tile,
                tile,
                *[whole for _ in bases],
            ],
            out_specs=whole,
            scratch_shapes=[
                pltpu.VMEM((8, share, rows), jnp.bfloat16),
                pltpu.VMEM((8, share, rows), jnp.bfloat16),
            ],
        ),
        out_shape=jax.ShapeDtypeStruct((8, share, rows), jnp.float32),
        compiler_params=pltpu.CompilerParams(vmem_limit_bytes=GRANT),
        cost_estimate=pl.CostEstimate(
            flops=2 * 16 * share * rows * rows,
            bytes_accessed=4 * rows * rows + (32 + 32 * (1 + len(bases))) * share * rows,
            transcendentals=0,
        ),
        name="advance",
    )(place, joined, in_hbm(kernels), in_hbm(inner), *map(in_hbm, bases))


def per_device(kernels, prestress, rates_hist, gain):
    moments, rows, scen = prestress.shape
    share = scen // 16
    core = lax.axis_index("k")
    yl = lax.axis_index("yl")
    plane = lax.axis_index("z")
    chip = lax.axis_index(CHIP)
    my_col = lax.axis_index(COL)
    order = lax.dynamic_index_in_dim(jnp.asarray(PLACES), chip, 0, keepdims=False)
    place = jnp.concatenate([core.reshape(1).astype(jnp.int32), order])

    def after(value):
        return lax.optimization_barrier((place, value))

    def reduced(partial_value, moment, beside):
        arrived = lax.all_to_all(partial_value, CHIP, 0, 0, tiled=True)
        _, (arrived, beside) = after((arrived, beside))
        traction = arrived.sum(axis=0) + load[moment - 1]
        return traction, jnp.tanh(gain * traction).astype(jnp.bfloat16), beside

    def crossing(rate):
        return moved(rate, lambda z, yl, u, k: (place_of(u, z), yl, z, k))

    def joining(crossed):
        copies = jnp.broadcast_to(crossed, (16, *crossed.shape))
        return lax.all_to_all(copies, ROW, 0, 0, tiled=True).reshape(8, 2, share, rows)

    mine, theirs = known(kernels, rates_hist, 1)
    now, (partial_value, tiles, hist) = after((mine + other_core(theirs), kernels, rates_hist))
    load = lax.dynamic_slice_in_dim(prestress, my_col * share, share, 2)
    load = jnp.swapaxes(load, 1, 2)
    inner = other_core(tiles)

    known_2 = known(tiles, hist, 2)
    traction_1, rate, known_2 = reduced(partial_value, 1, known_2)
    now, (crossed, tiles, hist) = after((crossing(rate), kernels, rates_hist))
    mine_2, theirs_2 = known_2[0], other_core(known_2[1])
    known_3 = known(tiles, hist, 3)
    known_3 = [known_3[0], other_core(known_3[1])]
    joined_1 = joining(crossed)
    partial_value = advance(joined_1, kernels, inner, 1, [mine_2, theirs_2], place)

    now, (partial_value, known_3) = after((partial_value, known_3))
    known_3 = advance(joined_1, kernels, inner, 2, known_3, now)
    traction_2, rate, known_3 = reduced(partial_value, 2, known_3)
    now, (crossed, tiles, hist) = after((crossing(rate), kernels, rates_hist))
    known_4 = known(tiles, hist, 4)
    from_1 = advance(joined_1, kernels, inner, 3, [], now)
    joined_2 = joining(crossed)
    partial_value = advance(joined_2, kernels, inner, 1, [known_3], place)

    now, (partial_value, known_4, from_1) = after((partial_value, known_4, from_1))
    traction_3, rate, _ = reduced(partial_value, 3, [])
    now, (crossed, known_4, from_1) = after((crossing(rate), known_4, from_1))
    known_4 = [known_4[0], other_core(known_4[1])]
    at = lax.dynamic_index_in_dim(now, 1 + plane, 0, keepdims=False)
    known_4 = advance(joined_2, kernels, inner, 2, [*known_4, from_1], now)
    joined_3 = joining(crossed)
    partial_value = advance(joined_3, kernels, inner, 1, [known_4], place)

    _, (partial_value, joined_list) = after((partial_value, [joined_1, joined_2, joined_3]))
    traction_4, rate, _ = reduced(partial_value, 4, [])
    tractions = [traction_1, traction_2, traction_3, traction_4]
    rate, tractions = lax.optimization_barrier((rate, tractions))
    last_rates = moved(rate, lambda z, yl, u, k: (u, k, z, yl))
    held = jnp.stack(
        [lax.dynamic_index_in_dim(joined, at, 0, keepdims=False) for joined in joined_list]
    )
    keep = lax.dynamic_index_in_dim(held, core, 1, keepdims=False)
    send = lax.dynamic_index_in_dim(held, 1 - core, 1, keepdims=False)
    early = jnp.where(yl == core, keep, other_core(send))
    rates = jnp.concatenate([early, last_rates[None]], axis=0)
    tractions = jnp.stack(tractions)
    return jnp.swapaxes(rates, 1, 2), jnp.swapaxes(tractions, 1, 2)


def solution(mesh):
    finer = Mesh(mesh.devices.reshape(SIZES), AXES)
    return jax.shard_map(
        per_device,
        mesh=finer,
        in_specs=(P(None, ROW, COL), P(None, ROW, None), P(None, COL, None), P(ROW)),
        out_specs=(P(None, COL, ROW), P(None, ROW, COL)),
        check_vma=False,
    )
```

```python
import jax
import jax.numpy as jnp
import numpy as np
from jax import lax
from jax.experimental import pallas as pl
from jax.experimental.pallas import tpu as pltpu
from jax.sharding import Mesh
from jax.sharding import PartitionSpec as P

AXES = ("z", "yl", "x", "yh", "k")
SIZES = (8, 2, 4, 2, 2)
ROW = ("z", "yl")
CHIP = ("x", "yh")
COL = ("x", "yh", "k")
STEP = {(2, 1): 0, (1, 1): 1, (3, 1): -1, (2, 0): 2, (0, 1): -2, (1, 0): 3, (3, 0): -3, (0, 0): 4}


def place_of(u, m):
    return (m + STEP[(u // 2 - m // 2) % 4, (u - m) % 2]) % 8


PLACES = np.array([[place_of(u, m) for u in range(8)] for m in range(8)], np.int32)

GRANT = 20 * 2**20


def pairs_of(move):
    def number(place):
        total = 0
        for size, at in zip(SIZES, place):
            total = total * size + at
        return total

    found = []
    for z in range(8):
        for yl in range(2):
            for u in range(8):
                for k in range(2):
                    to_z, to_yl, to_u, to_k = move(z, yl, u, k)
                    source = (z, yl, u // 2, u % 2, k)
                    target = (to_z, to_yl, to_u // 2, to_u % 2, to_k)
                    found.append((number(source), number(target)))
    return found


def moved(array, move):
    return lax.ppermute(array, AXES, pairs_of(move))


def other_core(array):
    return moved(array, lambda z, yl, u, k: (z, yl, u, 1 - k))


def in_hbm(array):
    return pltpu.with_memory_space_constraint(array, pltpu.HBM)


def known_kernel(kernel_ref, rates_ref, mine_ref, theirs_ref, total, turned):
    step = pl.program_id(0)
    product = jnp.dot(kernel_ref[0], rates_ref[0], preferred_element_type=jnp.float32)

    @pl.when(step == 0)
    def _():
        total[...] = product

    @pl.when(step > 0)
    def _():
        total[...] += product

    @pl.when(step == pl.num_programs(0) - 1)
    def _():
        turned[...] = total[...].T
        core = lax.axis_index("k")
        share = mine_ref.shape[1]
        for u in range(mine_ref.shape[0]):
            start = pl.multiple_of((2 * u + core) * share, share)
            mine_ref[u] = turned[pl.ds(start, share), :]
            start = pl.multiple_of((2 * u + 1 - core) * share, share)
            theirs_ref[u] = turned[pl.ds(start, share), :]


def known(kernels, rates_hist, moment):
    history, rows, scen = rates_hist.shape
    share = scen // 16
    out = jax.ShapeDtypeStruct((8, share, rows), jnp.float32)
    return pl.pallas_call(
        known_kernel,
        grid=(history,),
        in_specs=[
            pl.BlockSpec((1, rows, rows), lambda q: (moment - 1 + q, 0, 0)),
            pl.BlockSpec((1, rows, scen), lambda q: (history - 1 - q, 0, 0)),
        ],
        out_specs=[
            pl.BlockSpec((8, share, rows), lambda q: (0, 0, 0)),
            pl.BlockSpec((8, share, rows), lambda q: (0, 0, 0)),
        ],
        scratch_shapes=[
            pltpu.VMEM((rows, scen), jnp.float32),
            pltpu.VMEM((scen, rows), jnp.float32),
        ],
        out_shape=[out, out],
        compiler_params=pltpu.CompilerParams(vmem_limit_bytes=GRANT),
        cost_estimate=pl.CostEstimate(
            flops=2 * history * rows * rows * scen,
            bytes_accessed=2 * history * rows * (rows + scen) + 4 * rows * scen,
            transcendentals=0,
        ),
        name="known",
    )(in_hbm(kernels), in_hbm(rates_hist))


def advance_kernel(place_ref, joined_ref, own_ref, inner_ref, *refs):
    bases, out_ref, near, far = refs[:-3], refs[-3], refs[-2], refs[-1]
    core = place_ref[0]
    count, share, rows = out_ref.shape
    for u in range(count):
        at = place_ref[1 + u]
        near[u] = joined_ref[at, core]
        far[u] = joined_ref[at, 1 - core]
    parts = (((1,), (1,)), ((), ()))
    product = lax.dot_general(
        near[...].reshape(count * share, rows), own_ref[0], parts, preferred_element_type=jnp.float32
    )
    product += lax.dot_general(
        far[...].reshape(count * share, rows), inner_ref[0], parts, preferred_element_type=jnp.float32
    )
    product = product.reshape(count, share, rows)
    for base in bases:
        product += base[...]
    out_ref[...] = product


def advance(joined, kernels, inner, back, bases, place):
    _, _, share, rows = joined.shape
    tile = pl.BlockSpec((1, rows, rows), lambda j, c: (back - 1, 0, 0))
    whole = pl.BlockSpec((8, share, rows), lambda j, c: (0, 0, 0))
    return pl.pallas_call(
        advance_kernel,
        grid_spec=pltpu.PrefetchScalarGridSpec(
            num_scalar_prefetch=1,
            grid=(1,),
            in_specs=[
                pl.BlockSpec((8, 2, share, rows), lambda j, c: (0, 0, 0, 0)),
                tile,
                tile,
                *[whole for _ in bases],
            ],
            out_specs=whole,
            scratch_shapes=[
                pltpu.VMEM((8, share, rows), jnp.bfloat16),
                pltpu.VMEM((8, share, rows), jnp.bfloat16),
            ],
        ),
        out_shape=jax.ShapeDtypeStruct((8, share, rows), jnp.float32),
        compiler_params=pltpu.CompilerParams(vmem_limit_bytes=GRANT),
        cost_estimate=pl.CostEstimate(
            flops=2 * 16 * share * rows * rows,
            bytes_accessed=4 * rows * rows + (32 + 32 * (1 + len(bases))) * share * rows,
            transcendentals=0,
        ),
        name="advance",
    )(place, joined, in_hbm(kernels), in_hbm(inner), *map(in_hbm, bases))


def per_device(kernels, prestress, rates_hist, gain):
    moments, rows, scen = prestress.shape
    share = scen // 16
    core = lax.axis_index("k")
    yl = lax.axis_index("yl")
    plane = lax.axis_index("z")
    chip = lax.axis_index(CHIP)
    my_col = lax.axis_index(COL)
    order = lax.dynamic_index_in_dim(jnp.asarray(PLACES), chip, 0, keepdims=False)
    place = jnp.concatenate([core.reshape(1).astype(jnp.int32), order])

    def after(value):
        return lax.optimization_barrier((place, value))

    def reduced(partial_value, moment, beside):
        arrived = lax.all_to_all(partial_value, CHIP, 0, 0, tiled=True)
        _, (arrived, beside) = after((arrived, beside))
        total = arrived.sum(axis=0)
        traction = total + load[moment - 1]
        return total, jnp.tanh(gain * traction).astype(jnp.bfloat16), beside

    def crossing(rate):
        return moved(rate, lambda z, yl, u, k: (place_of(u, z), yl, z, k))

    def joining(crossed):
        copies = jnp.broadcast_to(crossed, (16, *crossed.shape))
        return lax.all_to_all(copies, ROW, 0, 0, tiled=True).reshape(8, 2, share, rows)

    mine, theirs = known(kernels, rates_hist, 1)
    now, (partial_value, tiles, hist) = after((mine + other_core(theirs), kernels, rates_hist))
    load = lax.dynamic_slice_in_dim(prestress, my_col * share, share, 2)
    load = jnp.swapaxes(load, 1, 2)
    inner = other_core(tiles)

    known_2 = known(tiles, hist, 2)
    total_1, rate, known_2 = reduced(partial_value, 1, known_2)
    now, (crossed, tiles, hist) = after((crossing(rate), kernels, rates_hist))
    mine_2, theirs_2 = known_2[0], other_core(known_2[1])
    known_3 = known(tiles, hist, 3)
    known_3 = [known_3[0], other_core(known_3[1])]
    joined_1 = joining(crossed)
    partial_value = advance(joined_1, kernels, inner, 1, [mine_2, theirs_2], place)

    now, (partial_value, known_3) = after((partial_value, known_3))
    known_3 = advance(joined_1, kernels, inner, 2, known_3, now)
    total_2, rate, known_3 = reduced(partial_value, 2, known_3)
    now, (crossed, tiles, hist) = after((crossing(rate), kernels, rates_hist))
    known_4 = known(tiles, hist, 4)
    from_1 = advance(joined_1, kernels, inner, 3, [], now)
    joined_2 = joining(crossed)
    partial_value = advance(joined_2, kernels, inner, 1, [known_3], place)

    now, (partial_value, known_4, from_1) = after((partial_value, known_4, from_1))
    total_3, rate, _ = reduced(partial_value, 3, [])
    now, (crossed, known_4, from_1) = after((crossing(rate), known_4, from_1))
    known_4 = [known_4[0], other_core(known_4[1])]
    at = lax.dynamic_index_in_dim(now, 1 + plane, 0, keepdims=False)
    known_4 = advance(joined_2, kernels, inner, 2, [*known_4, from_1], now)
    joined_3 = joining(crossed)
    partial_value = advance(joined_3, kernels, inner, 1, [known_4], place)

    _, (partial_value, joined_list) = after((partial_value, [joined_1, joined_2, joined_3]))
    total_4, rate, _ = reduced(partial_value, 4, [])
    rate, load = lax.optimization_barrier((rate, load))
    last_rates = moved(rate, lambda z, yl, u, k: (u, k, z, yl))
    held = jnp.stack(
        [lax.dynamic_index_in_dim(joined, at, 0, keepdims=False) for joined in joined_list]
    )
    keep = lax.dynamic_index_in_dim(held, core, 1, keepdims=False)
    send = lax.dynamic_index_in_dim(held, 1 - core, 1, keepdims=False)
    early = jnp.where(yl == core, keep, other_core(send))
    rates = jnp.concatenate([early, last_rates[None]], axis=0)
    tractions = jnp.stack([total_1, total_2, total_3, total_4]) + load
    return jnp.swapaxes(rates, 1, 2), jnp.swapaxes(tractions, 1, 2)


def solution(mesh):
    finer = Mesh(mesh.devices.reshape(SIZES), AXES)
    return jax.shard_map(
        per_device,
        mesh=finer,
        in_specs=(P(None, ROW, COL), P(None, ROW, None), P(None, COL, None), P(ROW)),
        out_specs=(P(None, COL, ROW), P(None, ROW, COL)),
        check_vma=False,
    )
```

```python
import jax
import jax.numpy as jnp
import numpy as np
from jax import lax
from jax.experimental import pallas as pl
from jax.experimental.pallas import tpu as pltpu
from jax.sharding import Mesh
from jax.sharding import PartitionSpec as P

AXES = ("z", "yl", "x", "yh", "k")
SIZES = (8, 2, 4, 2, 2)
ROW = ("z", "yl")
CHIP = ("x", "yh")
COL = ("x", "yh", "k")
STEP = {(2, 1): 0, (1, 1): 1, (3, 1): -1, (2, 0): 2, (0, 1): -2, (1, 0): 3, (3, 0): -3, (0, 0): 4}


def place_of(u, m):
    return (m + STEP[(u // 2 - m // 2) % 4, (u - m) % 2]) % 8


PLACES = np.array([[place_of(u, m) for u in range(8)] for m in range(8)], np.int32)

GRANT = 20 * 2**20


def pairs_of(move):
    def number(place):
        total = 0
        for size, at in zip(SIZES, place):
            total = total * size + at
        return total

    found = []
    for z in range(8):
        for yl in range(2):
            for u in range(8):
                for k in range(2):
                    to_z, to_yl, to_u, to_k = move(z, yl, u, k)
                    source = (z, yl, u // 2, u % 2, k)
                    target = (to_z, to_yl, to_u // 2, to_u % 2, to_k)
                    found.append((number(source), number(target)))
    return found


def moved(array, move):
    return lax.ppermute(array, AXES, pairs_of(move))


def other_core(array):
    return moved(array, lambda z, yl, u, k: (z, yl, u, 1 - k))


def in_hbm(array):
    return pltpu.with_memory_space_constraint(array, pltpu.HBM)


def known_kernel(kernel_ref, rates_ref, mine_ref, theirs_ref, total, turned):
    step = pl.program_id(0)
    product = jnp.dot(kernel_ref[0], rates_ref[0], preferred_element_type=jnp.float32)

    @pl.when(step == 0)
    def _():
        total[...] = product

    @pl.when(step > 0)
    def _():
        total[...] += product

    @pl.when(step == pl.num_programs(0) - 1)
    def _():
        turned[...] = total[...].T
        core = lax.axis_index("k")
        share = mine_ref.shape[1]
        for u in range(mine_ref.shape[0]):
            start = pl.multiple_of((2 * u + core) * share, share)
            mine_ref[u] = turned[pl.ds(start, share), :]
            start = pl.multiple_of((2 * u + 1 - core) * share, share)
            theirs_ref[u] = turned[pl.ds(start, share), :]


def known(kernels, rates_hist, moment):
    history, rows, scen = rates_hist.shape
    share = scen // 16
    out = jax.ShapeDtypeStruct((8, share, rows), jnp.float32)
    return pl.pallas_call(
        known_kernel,
        grid=(history,),
        in_specs=[
            pl.BlockSpec((1, rows, rows), lambda q: (moment - 1 + q, 0, 0)),
            pl.BlockSpec((1, rows, scen), lambda q: (history - 1 - q, 0, 0)),
        ],
        out_specs=[
            pl.BlockSpec((8, share, rows), lambda q: (0, 0, 0)),
            pl.BlockSpec((8, share, rows), lambda q: (0, 0, 0)),
        ],
        scratch_shapes=[
            pltpu.VMEM((rows, scen), jnp.float32),
            pltpu.VMEM((scen, rows), jnp.float32),
        ],
        out_shape=[out, out],
        compiler_params=pltpu.CompilerParams(vmem_limit_bytes=GRANT),
        cost_estimate=pl.CostEstimate(
            flops=2 * history * rows * rows * scen,
            bytes_accessed=2 * history * rows * (rows + scen) + 4 * rows * scen,
            transcendentals=0,
        ),
        name="known",
    )(in_hbm(kernels), in_hbm(rates_hist))


def advance_kernel(place_ref, joined_ref, own_ref, inner_ref, *refs):
    bases, out_ref, near, far = refs[:-3], refs[-3], refs[-2], refs[-1]
    core = place_ref[0]
    count, share, rows = out_ref.shape
    for u in range(count):
        at = place_ref[1 + u]
        near[u] = joined_ref[at, core]
        far[u] = joined_ref[at, 1 - core]
    parts = (((1,), (1,)), ((), ()))
    product = lax.dot_general(
        near[...].reshape(count * share, rows), own_ref[0], parts, preferred_element_type=jnp.float32
    )
    product += lax.dot_general(
        far[...].reshape(count * share, rows), inner_ref[0], parts, preferred_element_type=jnp.float32
    )
    product = product.reshape(count, share, rows)
    for base in bases:
        product += base[...]
    out_ref[...] = product


def advance(joined, kernels, inner, back, bases, place):
    _, _, share, rows = joined.shape
    tile = pl.BlockSpec((1, rows, rows), lambda j, c: (back - 1, 0, 0))
    whole = pl.BlockSpec((8, share, rows), lambda j, c: (0, 0, 0))
    return pl.pallas_call(
        advance_kernel,
        grid_spec=pltpu.PrefetchScalarGridSpec(
            num_scalar_prefetch=1,
            grid=(1,),
            in_specs=[
                pl.BlockSpec((8, 2, share, rows), lambda j, c: (0, 0, 0, 0)),
                tile,
                tile,
                *[whole for _ in bases],
            ],
            out_specs=whole,
            scratch_shapes=[
                pltpu.VMEM((8, share, rows), jnp.bfloat16),
                pltpu.VMEM((8, share, rows), jnp.bfloat16),
            ],
        ),
        out_shape=jax.ShapeDtypeStruct((8, share, rows), jnp.float32),
        compiler_params=pltpu.CompilerParams(vmem_limit_bytes=GRANT),
        cost_estimate=pl.CostEstimate(
            flops=2 * 16 * share * rows * rows,
            bytes_accessed=4 * rows * rows + (32 + 32 * (1 + len(bases))) * share * rows,
            transcendentals=0,
        ),
        name="advance",
    )(place, joined, in_hbm(kernels), in_hbm(inner), *map(in_hbm, bases))


def per_device(kernels, prestress, rates_hist, gain):
    moments, rows, scen = prestress.shape
    share = scen // 16
    core = lax.axis_index("k")
    yl = lax.axis_index("yl")
    plane = lax.axis_index("z")
    chip = lax.axis_index(CHIP)
    my_col = lax.axis_index(COL)
    order = lax.dynamic_index_in_dim(jnp.asarray(PLACES), chip, 0, keepdims=False)
    place = jnp.concatenate([core.reshape(1).astype(jnp.int32), order])

    def after(value):
        return lax.optimization_barrier((place, value))

    def reduced(partial_value, moment, beside):
        arrived = lax.all_to_all(partial_value, CHIP, 0, 0, tiled=True)
        _, (arrived, beside) = after((arrived, beside))
        total = arrived.sum(axis=0)
        traction = total + load[moment - 1]
        return total, jnp.tanh(gain * traction).astype(jnp.bfloat16), beside

    def crossing(rate):
        return moved(rate, lambda z, yl, u, k: (place_of(u, z), yl, z, k))

    def joining(crossed):
        copies = jnp.broadcast_to(crossed, (16, *crossed.shape))
        return lax.all_to_all(copies, ROW, 0, 0, tiled=True).reshape(8, 2, share, rows)

    mine, theirs = known(kernels, rates_hist, 1)
    now, (partial_value, tiles, hist) = after((mine + other_core(theirs), kernels, rates_hist))
    load = lax.dynamic_slice_in_dim(prestress, my_col * share, share, 2)
    load = jnp.swapaxes(load, 1, 2)
    inner = other_core(tiles)

    total_1, rate, _ = reduced(partial_value, 1, [])
    now, (crossed, tiles, hist) = after((crossing(rate), kernels, rates_hist))
    tiles, hist, known_2 = lax.optimization_barrier((tiles, hist, known(tiles, hist, 2)))
    mine_2, theirs_2 = known_2[0], other_core(known_2[1])
    known_3 = known(tiles, hist, 3)
    known_3 = [known_3[0], other_core(known_3[1])]
    joined_1 = joining(crossed)
    partial_value = advance(joined_1, kernels, inner, 1, [mine_2, theirs_2], place)

    now, (partial_value, known_3) = after((partial_value, known_3))
    known_3 = advance(joined_1, kernels, inner, 2, known_3, now)
    total_2, rate, known_3 = reduced(partial_value, 2, known_3)
    now, (crossed, tiles, hist) = after((crossing(rate), kernels, rates_hist))
    known_4 = known(tiles, hist, 4)
    from_1 = advance(joined_1, kernels, inner, 3, [], now)
    joined_2 = joining(crossed)
    partial_value = advance(joined_2, kernels, inner, 1, [known_3], place)

    now, (partial_value, known_4, from_1) = after((partial_value, known_4, from_1))
    total_3, rate, _ = reduced(partial_value, 3, [])
    now, (crossed, known_4, from_1) = after((crossing(rate), known_4, from_1))
    known_4 = [known_4[0], other_core(known_4[1])]
    at = lax.dynamic_index_in_dim(now, 1 + plane, 0, keepdims=False)
    known_4 = advance(joined_2, kernels, inner, 2, [*known_4, from_1], now)
    joined_3 = joining(crossed)
    partial_value = advance(joined_3, kernels, inner, 1, [known_4], place)

    _, (partial_value, joined_list) = after((partial_value, [joined_1, joined_2, joined_3]))
    total_4, rate, _ = reduced(partial_value, 4, [])
    rate, load = lax.optimization_barrier((rate, load))
    last_rates = moved(rate, lambda z, yl, u, k: (u, k, z, yl))
    held = jnp.stack(
        [lax.dynamic_index_in_dim(joined, at, 0, keepdims=False) for joined in joined_list]
    )
    keep = lax.dynamic_index_in_dim(held, core, 1, keepdims=False)
    send = lax.dynamic_index_in_dim(held, 1 - core, 1, keepdims=False)
    early = jnp.where(yl == core, keep, other_core(send))
    rates = jnp.concatenate([early, last_rates[None]], axis=0)
    tractions = jnp.stack([total_1, total_2, total_3, total_4]) + load
    return jnp.swapaxes(rates, 1, 2), jnp.swapaxes(tractions, 1, 2)


def solution(mesh):
    finer = Mesh(mesh.devices.reshape(SIZES), AXES)
    return jax.shard_map(
        per_device,
        mesh=finer,
        in_specs=(P(None, ROW, COL), P(None, ROW, None), P(None, COL, None), P(ROW)),
        out_specs=(P(None, COL, ROW), P(None, ROW, COL)),
        check_vma=False,
    )
```

```python
import jax
import jax.numpy as jnp
import numpy as np
from jax import lax
from jax.experimental import pallas as pl
from jax.experimental.pallas import tpu as pltpu
from jax.sharding import Mesh
from jax.sharding import PartitionSpec as P

AXES = ("z", "yl", "x", "yh", "k")
SIZES = (8, 2, 4, 2, 2)
ROW = ("z", "yl")
CHIP = ("x", "yh")
COL = ("x", "yh", "k")
STEP = {(2, 1): 0, (1, 1): 1, (3, 1): -1, (2, 0): 2, (0, 1): -2, (1, 0): 3, (3, 0): -3, (0, 0): 4}


def place_of(u, m):
    return (m + STEP[(u // 2 - m // 2) % 4, (u - m) % 2]) % 8


PLACES = np.array([[place_of(u, m) for u in range(8)] for m in range(8)], np.int32)

GRANT = 20 * 2**20


def pairs_of(move):
    def number(place):
        total = 0
        for size, at in zip(SIZES, place):
            total = total * size + at
        return total

    found = []
    for z in range(8):
        for yl in range(2):
            for u in range(8):
                for k in range(2):
                    to_z, to_yl, to_u, to_k = move(z, yl, u, k)
                    source = (z, yl, u // 2, u % 2, k)
                    target = (to_z, to_yl, to_u // 2, to_u % 2, to_k)
                    found.append((number(source), number(target)))
    return found


def moved(array, move):
    return lax.ppermute(array, AXES, pairs_of(move))


def other_core(array):
    return moved(array, lambda z, yl, u, k: (z, yl, u, 1 - k))


def in_hbm(array):
    return pltpu.with_memory_space_constraint(array, pltpu.HBM)


def known_kernel(kernel_ref, rates_ref, mine_ref, theirs_ref, total, turned):
    step = pl.program_id(0)
    product = jnp.dot(kernel_ref[0], rates_ref[0], preferred_element_type=jnp.float32)

    @pl.when(step == 0)
    def _():
        total[...] = product

    @pl.when(step > 0)
    def _():
        total[...] += product

    @pl.when(step == pl.num_programs(0) - 1)
    def _():
        turned[...] = total[...].T
        core = lax.axis_index("k")
        share = mine_ref.shape[1]
        for u in range(mine_ref.shape[0]):
            start = pl.multiple_of((2 * u + core) * share, share)
            mine_ref[u] = turned[pl.ds(start, share), :]
            start = pl.multiple_of((2 * u + 1 - core) * share, share)
            theirs_ref[u] = turned[pl.ds(start, share), :]


def known(kernels, rates_hist, moment):
    history, rows, scen = rates_hist.shape
    share = scen // 16
    out = jax.ShapeDtypeStruct((8, share, rows), jnp.float32)
    return pl.pallas_call(
        known_kernel,
        grid=(history,),
        in_specs=[
            pl.BlockSpec((1, rows, rows), lambda q: (moment - 1 + q, 0, 0)),
            pl.BlockSpec((1, rows, scen), lambda q: (history - 1 - q, 0, 0)),
        ],
        out_specs=[
            pl.BlockSpec((8, share, rows), lambda q: (0, 0, 0)),
            pl.BlockSpec((8, share, rows), lambda q: (0, 0, 0)),
        ],
        scratch_shapes=[
            pltpu.VMEM((rows, scen), jnp.float32),
            pltpu.VMEM((scen, rows), jnp.float32),
        ],
        out_shape=[out, out],
        compiler_params=pltpu.CompilerParams(vmem_limit_bytes=GRANT),
        cost_estimate=pl.CostEstimate(
            flops=2 * history * rows * rows * scen,
            bytes_accessed=2 * history * rows * (rows + scen) + 4 * rows * scen,
            transcendentals=0,
        ),
        name="known",
    )(in_hbm(kernels), in_hbm(rates_hist))


def advance_kernel(place_ref, joined_ref, own_ref, inner_ref, *refs):
    bases, out_ref, near, far = refs[:-3], refs[-3], refs[-2], refs[-1]
    core = place_ref[0]
    count, share, rows = out_ref.shape
    for u in range(count):
        at = place_ref[1 + u]
        near[u] = joined_ref[at, core]
        far[u] = joined_ref[at, 1 - core]
    parts = (((1,), (1,)), ((), ()))
    product = lax.dot_general(
        near[...].reshape(count * share, rows), own_ref[0], parts, preferred_element_type=jnp.float32
    )
    product += lax.dot_general(
        far[...].reshape(count * share, rows), inner_ref[0], parts, preferred_element_type=jnp.float32
    )
    product = product.reshape(count, share, rows)
    for base in bases:
        product += base[...]
    out_ref[...] = product


def advance(joined, kernels, inner, back, bases, place):
    _, _, share, rows = joined.shape
    tile = pl.BlockSpec((1, rows, rows), lambda j, c: (back - 1, 0, 0))
    whole = pl.BlockSpec((8, share, rows), lambda j, c: (0, 0, 0))
    return pl.pallas_call(
        advance_kernel,
        grid_spec=pltpu.PrefetchScalarGridSpec(
            num_scalar_prefetch=1,
            grid=(1,),
            in_specs=[
                pl.BlockSpec((8, 2, share, rows), lambda j, c: (0, 0, 0, 0)),
                tile,
                tile,
                *[whole for _ in bases],
            ],
            out_specs=whole,
            scratch_shapes=[
                pltpu.VMEM((8, share, rows), jnp.bfloat16),
                pltpu.VMEM((8, share, rows), jnp.bfloat16),
            ],
        ),
        out_shape=jax.ShapeDtypeStruct((8, share, rows), jnp.float32),
        compiler_params=pltpu.CompilerParams(vmem_limit_bytes=GRANT),
        cost_estimate=pl.CostEstimate(
            flops=2 * 16 * share * rows * rows,
            bytes_accessed=4 * rows * rows + (32 + 32 * (1 + len(bases))) * share * rows,
            transcendentals=0,
        ),
        name="advance",
    )(place, joined, in_hbm(kernels), in_hbm(inner), *map(in_hbm, bases))


def per_device(kernels, prestress, rates_hist, gain):
    moments, rows, scen = prestress.shape
    share = scen // 16
    core = lax.axis_index("k")
    yl = lax.axis_index("yl")
    plane = lax.axis_index("z")
    chip = lax.axis_index(CHIP)
    my_col = lax.axis_index(COL)
    order = lax.dynamic_index_in_dim(jnp.asarray(PLACES), chip, 0, keepdims=False)
    place = jnp.concatenate([core.reshape(1).astype(jnp.int32), order])

    def after(value):
        return lax.optimization_barrier((place, value))

    def reduced(partial_value, moment, beside):
        arrived = lax.all_to_all(partial_value, CHIP, 0, 0, tiled=True)
        _, (arrived, beside) = after((arrived, beside))
        total = arrived.sum(axis=0)
        traction = total + load[moment - 1]
        return total, jnp.tanh(gain * traction).astype(jnp.bfloat16), beside

    def crossing(rate):
        return moved(rate, lambda z, yl, u, k: (place_of(u, z), yl, z, k))

    def joining(crossed):
        copies = jnp.broadcast_to(crossed, (16, *crossed.shape))
        return lax.all_to_all(copies, ROW, 0, 0, tiled=True).reshape(8, 2, share, rows)

    mine, theirs = known(kernels, rates_hist, 1)
    now, (partial_value, tiles, hist) = after((mine + other_core(theirs), kernels, rates_hist))
    load = lax.dynamic_slice_in_dim(prestress, my_col * share, share, 2)
    load = jnp.swapaxes(load, 1, 2)

    total_1, rate, _ = reduced(partial_value, 1, [])
    now, (crossed, tiles, hist) = after((crossing(rate), kernels, rates_hist))
    inner = other_core(tiles)
    tiles, hist, known_2 = lax.optimization_barrier((tiles, hist, known(tiles, hist, 2)))
    mine_2, theirs_2 = known_2[0], other_core(known_2[1])
    known_3 = known(tiles, hist, 3)
    known_3 = [known_3[0], other_core(known_3[1])]
    joined_1 = joining(crossed)
    partial_value = advance(joined_1, kernels, inner, 1, [mine_2, theirs_2], place)

    now, (partial_value, known_3) = after((partial_value, known_3))
    known_3 = advance(joined_1, kernels, inner, 2, known_3, now)
    total_2, rate, known_3 = reduced(partial_value, 2, known_3)
    now, (crossed, tiles, hist) = after((crossing(rate), kernels, rates_hist))
    known_4 = known(tiles, hist, 4)
    from_1 = advance(joined_1, kernels, inner, 3, [], now)
    joined_2 = joining(crossed)
    partial_value = advance(joined_2, kernels, inner, 1, [known_3], place)

    now, (partial_value, known_4, from_1) = after((partial_value, known_4, from_1))
    total_3, rate, _ = reduced(partial_value, 3, [])
    now, (crossed, known_4, from_1) = after((crossing(rate), known_4, from_1))
    known_4 = [known_4[0], other_core(known_4[1])]
    at = lax.dynamic_index_in_dim(now, 1 + plane, 0, keepdims=False)
    known_4 = advance(joined_2, kernels, inner, 2, [*known_4, from_1], now)
    joined_3 = joining(crossed)
    partial_value = advance(joined_3, kernels, inner, 1, [known_4], place)

    _, (partial_value, joined_list) = after((partial_value, [joined_1, joined_2, joined_3]))
    total_4, rate, _ = reduced(partial_value, 4, [])
    rate, load = lax.optimization_barrier((rate, load))
    last_rates = moved(rate, lambda z, yl, u, k: (u, k, z, yl))
    held = jnp.stack(
        [lax.dynamic_index_in_dim(joined, at, 0, keepdims=False) for joined in joined_list]
    )
    keep = lax.dynamic_index_in_dim(held, core, 1, keepdims=False)
    send = lax.dynamic_index_in_dim(held, 1 - core, 1, keepdims=False)
    early = jnp.where(yl == core, keep, other_core(send))
    rates = jnp.concatenate([early, last_rates[None]], axis=0)
    tractions = jnp.stack([total_1, total_2, total_3, total_4]) + load
    return jnp.swapaxes(rates, 1, 2), jnp.swapaxes(tractions, 1, 2)


def solution(mesh):
    finer = Mesh(mesh.devices.reshape(SIZES), AXES)
    return jax.shard_map(
        per_device,
        mesh=finer,
        in_specs=(P(None, ROW, COL), P(None, ROW, None), P(None, COL, None), P(ROW)),
        out_specs=(P(None, COL, ROW), P(None, ROW, COL)),
        check_vma=False,
    )
```
